32 devices in a mesh: survey: 2 (over x), gx: 16 (over z, y, core).
Axes of the slice: x: 2, y: 2, z: 4, core: 2. Of those that a mesh axis runs over, the one named last changes fastest.
Arguments:
- courant: float32 [256, 256, 256], P('gx', 'survey'), parts along dimension 1, may hold values from 0.06 to 0.24
- sketches: bfloat16 [4, 4, 256, 128, 256], P('survey', None, 'gx'), parts along dimension 0, may hold values from -6 to 6
- probes: float32 [4, 8, 4], P('survey'), parts along dimension 0, may hold values from -6 to 6
- source_spot: int32 [4, 3], P('survey'), parts along dimension 0, may hold values from 0 to 255, as said below
- wavelet: float32 [4, 8], P('survey'), parts along dimension 0, may hold values from -48 to 48
- adjoint_before: float32 [4, 256, 128, 256], P('survey', 'gx'), parts along dimension 0, may hold values from -2 to 2
- adjoint_start: float32 [4, 256, 128, 256], P('survey', 'gx'), parts along dimension 0, may hold values from -2 to 2
Outputs:
- imaging: float32 [256, 256, 256], P('gx', 'survey'), parts along dimension 1
- adjoint_end: float32 [4, 256, 128, 256], P('survey', 'gx'), parts along dimension 0
The draws below stay inside these ranges and needn't reach their ends.
There are 2 independent parts, one for each index of `survey`. The reference program is written for one: setup_inputs(seed, part) draws one part's arguments, and reference() takes and returns one part's arrays. A program takes and returns all parts, laid end to end along the dimension named above; each array names one. Nothing has to cross between parts.
Inputs may be any that keep to these rules, and one draw needn't show every extreme that they name: `source_spot`: column 0 lies below 256, column 1 below 128, column 2 below 256.
All inputs are finite; a program needn't handle non-finite values.
Results may differ from the reference program's by a relative error of at most 0.0003.
Values sent between devices are 32-bit elements; how exact they have to be, the bound alone decides.
No kernel may reach another device: no remote copies, remote signals or barrier semaphores. Data moves between devices by JAX's collectives and lax.ppermute only.
A program may use at most 192 MiB of HBM per device.

```python
import jax
import jax.numpy as jnp

NY = 128
NZ = 256
SHOTS = 2
STEPS = 8
FRAMES = 4
NX = 256


def draw_source_spot(key, part):
    first = jax.random.randint(jax.random.fold_in(key, 11), (SHOTS, 1), 0, NX)
    second = jax.random.randint(jax.random.fold_in(key, 12), (SHOTS, 1), 0, NY)
    third = jax.random.randint(jax.random.fold_in(key, 13), (SHOTS, 1), 0, NZ)
    spots = jnp.concatenate([first, second, third], axis=1).astype(jnp.int32)
    extents = [NX, NY, NZ]
    longest = max(extents)
    for column in range(3):
        if extents[column] == longest:
            spots = spots.at[0, column].set(extents[column] - 1)
    return spots.astype(jnp.int32)


def levels(rng, dims, cuts, least, top_value):
    level, own = 1.0, jax.random.fold_in(rng, 6)
    for axis_at, blocks in cuts:
        heights = jnp.exp(jax.random.uniform(jax.random.fold_in(own, axis_at), (blocks,), jnp.float32, least / len(cuts), top_value / len(cuts)))
        level = level * jnp.repeat(heights, dims[axis_at] // blocks).reshape([-1 if axis == axis_at else 1 for axis in range(len(dims))])
    return level


def normal_values(key, shape, width, limit, split=(), held_as=jnp.bfloat16):
    result = jax.random.normal(key, shape, jnp.float32) * width
    if len(split) > 0:
        result = levels(key, shape, split, -0.22, 0.18) * result
    return jnp.clip(result, min=-limit, max=limit).astype(held_as)


def setup_inputs(seed: int = 0, part: int = 0) -> dict:
    key_of = jax.random.split(jax.random.key(seed), 8)
    part_keys = jax.random.split(jax.random.fold_in(key_of[7], part), 8)
    return {
        "courant": jnp.clip(0.06 + 0.179999996 * jax.random.uniform(part_keys[0], (NX, NY, NZ), jnp.float32) ** levels(part_keys[0], (NX, NY, NZ), ((0, 16),), -0.2, 0.2), 0.06, 0.24),
        "sketches": normal_values(part_keys[1], (SHOTS, FRAMES, NX, NY, NZ), 1.0, 6.0, ((2, 16),)),
        "probes": normal_values(part_keys[2], (SHOTS, STEPS, FRAMES), 1.0, 6.0, (), jnp.float32),
        "source_spot": draw_source_spot(jax.random.fold_in(jax.random.fold_in(key_of[7], part), 71), part),
        "wavelet": normal_values(part_keys[4], (SHOTS, STEPS), 8.0, 48.0, (), jnp.float32),
        "adjoint_before": normal_values(part_keys[5], (SHOTS, NX, NY, NZ), 0.3, 2.0, ((1, 16),), jnp.float32),
        "adjoint_start": normal_values(part_keys[6], (SHOTS, NX, NY, NZ), 0.3, 2.0, ((1, 16),), jnp.float32),
    }


def laplace_center(padded):
    center = padded[:, 2:-2]
    total = -(padded[:, :-4] + padded[:, 4:]) / 12.0 + (padded[:, 1:-3] + padded[:, 3:-1]) * (4.0 / 3.0) - 2.5 * center
    wide_y = jnp.pad(center, ((0, 0), (0, 0), (2, 2), (0, 0)))
    total = total - (wide_y[:, :, :-4] + wide_y[:, :, 4:]) / 12.0 + (wide_y[:, :, 1:-3] + wide_y[:, :, 3:-1]) * (4.0 / 3.0) - 2.5 * center
    wide_z = jnp.pad(center, ((0, 0), (0, 0), (0, 0), (2, 2)))
    total = total - (wide_z[:, :, :, :-4] + wide_z[:, :, :, 4:]) / 12.0 + (wide_z[:, :, :, 1:-3] + wide_z[:, :, :, 3:-1]) * (4.0 / 3.0) - 2.5 * center
    return total


def inject(spots, amplitude, coords, breadth, height):
    plane = (coords[None, :] == spots[:, 0:1]).astype(jnp.float32)
    row_hit = (jnp.arange(breadth, dtype=jnp.int32)[None, :] == spots[:, 1:2]).astype(jnp.float32)
    col_hit = (jnp.arange(height, dtype=jnp.int32)[None, :] == spots[:, 2:3]).astype(jnp.float32)
    return amplitude[:, None, None, None] * plane[:, :, None, None] * row_hit[:, None, :, None] * col_hit[:, None, None, :]


def reference(courant, sketches, probes, source_spot, wavelet, adjoint_before, adjoint_start):
    previous = adjoint_before
    current = adjoint_start
    coords = jnp.arange(NX, dtype=jnp.int32)
    image = jnp.zeros((NX, NY, NZ), jnp.float32)
    lighting = jnp.zeros((NX, NY, NZ), jnp.float32)
    for instant in range(STEPS):
        padded = jnp.pad(current, ((0, 0), (2, 2), (0, 0), (0, 0)))
        advanced = 2.0 * current - previous + courant[None] * laplace_center(padded) + inject(source_spot, wavelet[:, instant], coords, NY, NZ)
        previous = current
        current = advanced
        weighted = jnp.zeros_like(current)
        for sketch_index in range(FRAMES):
            weighted = weighted + probes[:, instant, sketch_index][:, None, None, None] * sketches[:, sketch_index].astype(jnp.float32)
        image = image + jnp.sum(weighted * current, axis=0)
        lighting = lighting + jnp.sum(current * current, axis=0)
    largest = jnp.max(lighting)
    return image / (lighting + 0.1 * largest), current
```

```python
import functools

import jax
import jax.numpy as jnp
from jax import lax
from jax.experimental import pallas as pl
from jax.experimental.pallas import tpu as pltpu
from jax.sharding import PartitionSpec as P

F32 = jnp.float32
BF16 = jnp.bfloat16
VMEM = pl.BlockSpec(memory_space=pltpu.VMEM)
SMEM = pl.BlockSpec(memory_space=pltpu.SMEM)
ANY = pl.BlockSpec(memory_space=pl.ANY)
EDGE = 2


def held(*dims):
    return pltpu.VMEM(dims, F32)


def in_hbm(array):
    return pltpu.with_memory_space_constraint(array, pltpu.HBM)


def call(body, outs, ins, aliases=None, scratch=(), flops=0, moved=0, limit=6 << 20):
    return pl.pallas_call(
        body,
        out_shape=outs,
        in_specs=ins,
        out_specs=jax.tree.map(lambda _: VMEM, outs),
        scratch_shapes=scratch,
        input_output_aliases=aliases or {},
        compiler_params=pltpu.CompilerParams(vmem_limit_bytes=limit),
        cost_estimate=pl.CostEstimate(flops=flops, bytes_accessed=moved, transcendentals=0),
    )


def orientation(planes, far):
    odd = lax.rem(lax.axis_index("gx"), 2)
    sign = 2 * odd - 1
    base = (1 - odd) * (planes - 1)
    return (base + sign * (planes - 1), -sign) if far else (base, sign)


def pack_body(far, shots, planes, start, *refs):
    outs, sems = refs[:-1], refs[-1]
    base, sign = orientation(planes, far)
    started = []
    for s in range(shots):
        for d in range(EDGE):
            target = outs[s].at[d] if far else outs[0].at[s * EDGE + d]
            copy = pltpu.make_async_copy(start.at[s, base + sign * d], target, sems.at[s * EDGE + d])
            copy.start()
            started.append(copy)
    for copy in started:
        copy.wait()


def dot(a, b):
    return lax.dot_general(a, b, (((1,), (0,)), ((), ())), preferred_element_type=F32)


def advance(down2, down1, mid, up1, up2, last, scaled, along_z, along_y):
    high = mid.astype(BF16)
    low = (mid - high.astype(F32)).astype(BF16)
    total = dot(high, along_z) + dot(low, along_z) + dot(along_y, jnp.concatenate([high, low], axis=0))
    total = total + (16.0 * (down1 + up1) - (down2 + up2))
    return 2.0 * mid - last + scaled * total


def inject(ref, here, row, column, amount):
    @pl.when(here)
    def _():
        top = pl.multiple_of((row // 8) * 8, 8)
        tile = ref[pl.ds(top, 8), :]
        rows = lax.broadcasted_iota(jnp.int32, tile.shape, 0)
        columns = lax.broadcasted_iota(jnp.int32, tile.shape, 1)
        ref[pl.ds(top, 8), :] = tile + jnp.where((rows == row - top) & (columns == column), amount, 0.0)


def source(planes, spots, wavelet, instant, s, base, sign, target, low, high):
    plane = spots[s, 0] - lax.axis_index("gx") * planes
    own = (plane - base) * sign
    inject(
        target.at[s, jnp.clip(plane, 0, planes - 1)], (own >= low) & (own < high),
        spots[s, 1], spots[s, 2], wavelet[s, instant],
    )


def main_body(shots, planes, frames, instant, spots, wavelet, probes, field, last, courant, along_z, along_y, ghost, *refs):
    refs = list(refs)
    images = instant > 0
    adds = instant > 1
    if images:
        sketches = refs.pop(0)
    if adds:
        image_in, light_in = refs[:2]
        del refs[:2]
    ahead, send = refs[:2]
    del refs[:2]
    base, sign = orientation(planes, False)

    def at(j):
        return base + sign * j

    def now(s, j):
        return ghost[s * EDGE - 1 - j] if isinstance(j, int) and j < 0 else field[s, at(j)]

    def step(j):
        scaled = courant[at(j)] * (1.0 / 12.0)
        for s in range(shots):
            five = [now(s, j + d) for d in (-2, -1, 0, 1, 2)]
            ahead[s, at(j)] = advance(*five, last[s, at(j)], scaled, along_z[...], along_y[...])

    def body(j, carry):
        step(j)
        return carry

    for j in range(EDGE):
        step(j)
    lax.fori_loop(EDGE, planes - EDGE, body, 0, unroll=2)
    for s in range(shots):
        source(planes, spots, wavelet, instant, s, base, sign, ahead, 0, planes - EDGE)
    for s in range(shots):
        for d in range(EDGE):
            send[s * EDGE + d] = ahead[s, at(d)]
    if images:
        add_image(shots, planes, frames, (instant - 1,), (field,), probes, sketches,
                  (image_in, light_in) if adds else None, refs[0], refs[1])


def far_body(shot, planes, instant, spots, wavelet, probes, field, last, courant, along_z, along_y, ghost, partial, ahead, *refs):
    base, sign = orientation(planes, True)
    index = lax.axis_index("gx")
    inner = (index > 0) & (index < lax.axis_size("gx") - 1)

    def at(k):
        return base + sign * k

    def now(k):
        return jnp.where(inner, ghost[-1 - k], 0.0) if k < 0 else field[shot, at(k)]

    for k in range(EDGE):
        five = [now(k + d) for d in (-2, -1, 0, 1, 2)]
        ahead[shot, at(k)] = advance(
            *five, last[shot, at(k)], courant[at(k)] * (1.0 / 12.0), along_z[...], along_y[...]
        )
    source(planes, spots, wavelet, instant, shot, base, sign, ahead, 0, EDGE)
    if refs:
        for k in range(EDGE):
            refs[0][k] = ahead[shot, at(k)]


def add_image(shots, planes, frames, instants, fields, probes, sketches, before, image_out, light_out):
    breadth = image_out.shape[1]
    chunk = 16
    per = breadth // chunk

    def body(number, carry):
        p = number // per
        rows = pl.ds(pl.multiple_of((number % per) * chunk, chunk), chunk)
        image = light = None
        if before is not None:
            image, light = before[0][p, rows, :], before[1][p, rows, :]
        for s in range(shots):
            drawn = [sketches[s, k, p, rows, :].astype(F32) for k in range(frames)]
            for instant, field in zip(instants, fields):
                value = field[s, p, rows, :]
                weighted = probes[s, instant, 0] * drawn[0]
                for k in range(1, frames):
                    weighted = weighted + probes[s, instant, k] * drawn[k]
                image = weighted * value if image is None else image + weighted * value
                light = value * value if light is None else light + value * value
        image_out[p, rows, :] = image
        light_out[p, rows, :] = light
        return carry

    lax.fori_loop(0, planes * per, body, 0, unroll=2)


def last_body(shots, planes, frames, instant, probes, sketches, field, image_in, light_in, image_out, light_out, most):
    add_image(shots, planes, frames, (instant,), (field,), probes, sketches, (image_in, light_in), image_out, light_out)
    breadth, height = light_out.shape[1:]

    def highest(p):
        return jnp.max(light_out[p].reshape(breadth // 8, 8, height), axis=0)

    most[...] = lax.fori_loop(1, planes, lambda p, so_far: jnp.maximum(so_far, highest(p)), highest(0))


def divide_body(planes, image, light, most, out):
    largest = 0.1 * jnp.max(most[...])

    def body(p, carry):
        out[p] = image[p] / (light[p] + largest)
        return carry

    lax.fori_loop(0, planes, body, 0)


def per_device(courant, sketches, probes, source_spot, wavelet, adjoint_before, adjoint_start):
    shots, planes, breadth, height = adjoint_start.shape
    frames, steps = sketches.shape[1], wavelet.shape[1]
    count, areas = lax.axis_size("gx"), lax.axis_size("survey")

    def band(size, center):
        apart = jnp.abs(jnp.arange(size)[:, None] - jnp.arange(size)[None, :])
        return jnp.where(apart == 0, center, jnp.where(apart == 1, 16.0, jnp.where(apart == 2, -1.0, 0.0))).astype(BF16)

    along_z = band(height, -60.0)
    along_y = band(breadth, -30.0)
    along_y = jnp.concatenate([along_y, along_y], axis=1)

    near_pairs = [(i, i ^ 1) for i in range(count)]
    far_pairs = []
    for area in range(areas):
        for i in range(count):
            other = i + 1 if i % 2 else i - 1
            if 0 <= other < count:
                far_pairs.append((area * count + i, area * count + other))
            elif areas % 2 == 0:
                far_pairs.append((area * count + i, (area ^ 1) * count + i))
    plane_bytes = 4 * breadth * height
    whole = held(shots, planes, breadth, height)
    still = held(planes, breadth, height)
    edge = held(EDGE, breadth, height)
    both = held(shots * EDGE, breadth, height)

    def to_far(planes_out):
        return lax.ppermute(planes_out, ("survey", "gx"), far_pairs)

    def to_near(planes_out):
        return lax.ppermute(planes_out, "gx", near_pairs)

    def pack(far):
        return call(
            functools.partial(pack_body, far, shots, planes),
            (edge,) * shots if far else (both,), [ANY], scratch=[pltpu.SemaphoreType.DMA((shots * EDGE,))],
            moved=4 * shots * plane_bytes,
        )(in_hbm(adjoint_start))

    far = [to_far(part) for part in pack(True)]
    near = to_near(pack(False)[0])
    field, last = adjoint_start, adjoint_before
    images = ()
    for instant in range(steps):
        closing = instant == steps - 1
        shared = [source_spot, wavelet, probes, field, last, courant, along_z, along_y]
        specs = [SMEM] * 3 + [VMEM] * 5
        extra, extra_specs, aliases, outs = [], [], {}, (whole, both)
        if instant > 0:
            extra, extra_specs = [sketches, *images], [VMEM] * (1 + len(images))
            outs = outs + (still, still)
        if images:
            at = len(shared) + 2
            aliases = {at: 2, at + 1: 3}
        ahead, near_sent, *images = call(
            functools.partial(main_body, shots, planes, frames, instant), outs,
            specs + [VMEM] + extra_specs, aliases=aliases,
            flops=2 * planes * shots * breadth * height * 512, moved=8 * planes * shots * plane_bytes,
        )(*shared, near, *extra)
        if not closing:
            near = to_near(near_sent)
        for shot in range(shots):
            at = len(shared) + 1
            ahead, *sent = call(
                functools.partial(far_body, shot, planes, instant),
                (whole,) if closing else (whole, edge), specs + [VMEM] * 2, aliases={at: 0},
                flops=4 * breadth * height * 512, moved=16 * plane_bytes,
            )(*shared, far[shot], ahead)
            if not closing:
                far[shot] = to_far(sent[0])
        field, last = ahead, field
    image, light, most = call(
        functools.partial(last_body, shots, planes, frames, steps - 1),
        (still, still, held(8, height)), [SMEM] + [VMEM] * 4, aliases={3: 0, 4: 1},
        moved=8 * planes * shots * plane_bytes,
    )(probes, sketches, field, *images)
    reach = 1
    while reach < count:
        most = jnp.maximum(most, lax.ppermute(most, "gx", [(i, i ^ reach) for i in range(count)]))
        reach *= 2
    result = call(
        functools.partial(divide_body, planes), jax.ShapeDtypeStruct((planes, breadth, height), F32), [VMEM] * 3,
        moved=3 * planes * plane_bytes,
    )(image, light, most)
    return result, field


def solution(mesh):
    placed = (
        P("gx", "survey", None),
        P("survey", None, "gx", None, None),
        P("survey", None, None),
        P("survey", None),
        P("survey", None),
        P("survey", "gx", None, None),
        P("survey", "gx", None, None),
    )
    return jax.shard_map(
        per_device,
        mesh=mesh,
        in_specs=placed,
        out_specs=(P("gx", "survey", None), P("survey", "gx", None, None)),
        check_vma=False,
    )
```

```python
import functools

import jax
import jax.numpy as jnp
from jax import lax
from jax.experimental import pallas as pl
from jax.experimental.pallas import tpu as pltpu
from jax.sharding import PartitionSpec as P

F32 = jnp.float32
BF16 = jnp.bfloat16
VMEM = pl.BlockSpec(memory_space=pltpu.VMEM)
SMEM = pl.BlockSpec(memory_space=pltpu.SMEM)
ANY = pl.BlockSpec(memory_space=pl.ANY)
EDGE = 2
CHUNKS = 4


def held(*dims):
    return pltpu.VMEM(dims, F32)


def in_hbm(array):
    return pltpu.with_memory_space_constraint(array, pltpu.HBM)


def call(body, outs, ins, aliases=None, scratch=(), flops=0, moved=0, limit=6 << 20, out_spec=VMEM):
    return pl.pallas_call(
        body,
        out_shape=outs,
        in_specs=ins,
        out_specs=jax.tree.map(lambda _: out_spec, outs),
        scratch_shapes=scratch,
        input_output_aliases=aliases or {},
        compiler_params=pltpu.CompilerParams(vmem_limit_bytes=limit),
        cost_estimate=pl.CostEstimate(flops=flops, bytes_accessed=moved, transcendentals=0),
    )


def orientation(planes, far):
    odd = lax.rem(lax.axis_index("gx"), 2)
    sign = 2 * odd - 1
    base = (1 - odd) * (planes - 1)
    return (base + sign * (planes - 1), -sign) if far else (base, sign)


def pack_body(shots, planes, start, *refs):
    outs, sems = refs[:-1], refs[-1]
    started = []
    for far in (True, False):
        base, sign = orientation(planes, far)
        for s in range(shots):
            for d in range(EDGE):
                target = outs[s].at[d] if far else outs[shots].at[s * EDGE + d]
                copy = pltpu.make_async_copy(start.at[s, base + sign * d], target, sems.at[len(started)])
                copy.start()
                started.append(copy)
    for copy in started:
        copy.wait()


def band(rows, columns, center):
    row = lax.broadcasted_iota(jnp.int32, (rows, columns), 0)
    column = lax.broadcasted_iota(jnp.int32, (rows, columns), 1)
    apart = jnp.abs(row - lax.rem(column, rows))
    return jnp.where(apart == 0, center, jnp.where(apart == 1, 16.0, jnp.where(apart == 2, -1.0, 0.0))).astype(BF16)


def tables_body(planes, spots, wavelet, probes, along_z, along_y, weights, force, edge_force, spot_mask, spot_plane):
    along_z[...] = band(*along_z.shape, -60.0)
    along_y[...] = band(*along_y.shape, -30.0)
    steps, shots, frames = weights.shape[:3]
    base, sign = orientation(planes, False)
    tile = weights.shape[3:]
    for s in range(shots):
        own = (spots[s, 0] - lax.axis_index("gx") * planes - base) * sign
        spot_plane[s] = jnp.full(tile, own, jnp.int32).astype(F32)
        rows = lax.broadcasted_iota(jnp.int32, spot_mask.shape[1:], 0)
        columns = lax.broadcasted_iota(jnp.int32, spot_mask.shape[1:], 1)
        spot_mask[s] = jnp.where((rows == spots[s, 1]) & (columns == spots[s, 2]), 1.0, 0.0)
        for t in range(steps):
            force[t, s] = jnp.full(tile, wavelet[s, t], F32)
            for k in range(EDGE):
                edge_force[t, s, k] = jnp.full(tile, jnp.where(own == planes - 1 - k, wavelet[s, t], 0.0), F32)
            for k in range(frames):
                weights[t, s, k] = jnp.full(tile, probes[s, t, k], F32)


def spread(plane, tile):
    rows, columns = plane.shape
    height, width = tile.shape
    parts = [
        (plane[:, at : at + width].reshape(rows // height, height, width) * tile[None]).reshape(rows, width)
        for at in range(0, columns, width)
    ]
    return jnp.concatenate(parts, axis=1)


def dot(a, b):
    return lax.dot_general(a, b, (((1,), (0,)), ((), ())), preferred_element_type=F32)


def advance(down2, down1, mid, up1, up2, last, scaled, along_z, along_y):
    high = mid.astype(BF16)
    low = (mid - high.astype(F32)).astype(BF16)
    total = dot(high, along_z) + dot(low, along_z) + dot(along_y, jnp.concatenate([high, low], axis=0))
    total = total + (16.0 * (down1 + up1) - (down2 + up2))
    return 2.0 * mid - last + scaled * total


def main_body(shots, planes, instant, closing, *refs):
    refs = list(refs)

    def take(count):
        taken = refs[:count]
        del refs[:count]
        return taken

    opening = instant == 0
    along_z, along_y, spot_plane, spot_mask, force, ghost = take(6)
    if opening:
        sources = take(4)
        ahead, send, field, last, courant, sketches = take(6)
        sems = refs[0]
        slab = planes // CHUNKS
        odd = lax.rem(lax.axis_index("gx"), 2)
        copies = []
        for c in range(CHUNKS):
            first = odd * (c * slab) + (1 - odd) * (planes - slab - c * slab)
            span = pl.ds(first, slab)
            copies.append([
                pltpu.make_async_copy(sources[0].at[:, span], field.at[:, span], sems.at[3 * c]),
                pltpu.make_async_copy(sources[1].at[:, span], last.at[:, span], sems.at[3 * c + 1]),
                pltpu.make_async_copy(sources[2].at[span], courant.at[span], sems.at[3 * c + 2]),
            ])
            for copy in copies[-1]:
                copy.start()
        drawing = pltpu.make_async_copy(sources[3], sketches, sems.at[3 * CHUNKS])
        drawing.start()
    else:
        field, last, courant, weights, sketches = take(5)
        before = take(2) if len(refs) > 4 else None
        ahead, send, image, light = take(4)
    base, sign = orientation(planes, False)

    def at(j):
        return base + sign * j

    def now(s, j):
        return ghost[s * EDGE - 1 - j] if isinstance(j, int) and j < 0 else field[s, at(j)]

    def step(j):
        scaled = courant[at(j)] * (1.0 / 12.0)
        for s in range(shots):
            five = [now(s, j + d) for d in (-2, -1, 0, 1, 2)]
            ahead[s, at(j)] = advance(*five, last[s, at(j)], scaled, along_z[...], along_y[...])

    def body(j, carry):
        step(j)
        return carry

    if opening:
        for c in range(CHUNKS):
            for copy in copies[c]:
                copy.wait()
            if c == 0:
                for j in range(EDGE):
                    step(j)
            low, high = (EDGE, slab - EDGE) if c == 0 else (c * slab - EDGE, (c + 1) * slab - EDGE)
            lax.fori_loop(low, high, body, 0, unroll=2)
    else:
        for j in range(EDGE):
            step(j)
        lax.fori_loop(EDGE, planes - EDGE, body, 0, unroll=2)
    for s in range(shots):
        own = jnp.max(spot_plane[s]).astype(jnp.int32)

        @pl.when((own >= 0) & (own < planes - EDGE))
        def _():
            plane = jnp.clip(at(own), 0, planes - 1)
            ahead[s, plane] = ahead[s, plane] + spread(spot_mask[s], force[instant, s])

    if not closing:
        for s in range(shots):
            for d in range(EDGE):
                send[s * EDGE + d] = ahead[s, at(d)]
    if opening:
        drawing.wait()
    else:
        done = [(field, weights.at[instant - 1])]
        if closing:
            odd = lax.rem(lax.axis_index("gx"), 2)
            ready = done + [(ahead, weights.at[instant])]
            add_image((1 - odd) * EDGE, planes - EDGE, ready, sketches, before, image, light)
            add_image(odd * (planes - EDGE), EDGE, done, sketches, before, image, light)
        else:
            add_image(0, planes, done, sketches, before, image, light)


def far_body(instant, shot, planes, along_z, along_y, edge_force, spot_mask, ghost, field, last, courant, partial, ahead, *refs):
    base, sign = orientation(planes, True)
    index = lax.axis_index("gx")
    inner = (index > 0) & (index < lax.axis_size("gx") - 1)

    def at(k):
        return base + sign * k

    def now(k):
        return jnp.where(inner, ghost[-1 - k], 0.0) if k < 0 else field[shot, at(k)]

    for k in range(EDGE):
        five = [now(k + d) for d in (-2, -1, 0, 1, 2)]
        value = advance(*five, last[shot, at(k)], courant[at(k)] * (1.0 / 12.0), along_z[...], along_y[...])
        value = value + spread(spot_mask[shot], edge_force[instant, shot, k])
        ahead[shot, at(k)] = value
        if refs:
            refs[0][k] = value


def add_image(low, count, steps, sketches, before, image_out, light_out):
    shots, frames = sketches.shape[:2]
    breadth, height = image_out.shape[1:]
    rows, columns = 16, 128
    down, across = breadth // rows, height // columns

    def tiles(value):
        return value.reshape(rows // 8, 8, columns)

    def body(number, carry):
        p = low + number // down
        row = pl.ds(pl.multiple_of((number % down) * rows, rows), rows)
        for c in range(across):
            column = pl.ds(c * columns, columns)
            image = light = None
            if before is not None:
                image, light = tiles(before[0][p, row, column]), tiles(before[1][p, row, column])
            for s in range(shots):
                drawn = [tiles(sketches[s, k, p, row, column].astype(F32)) for k in range(frames)]
                for field, weights in steps:
                    value = tiles(field[s, p, row, column])
                    weighted = weights[s, 0][None] * drawn[0]
                    for k in range(1, frames):
                        weighted = weighted + weights[s, k][None] * drawn[k]
                    image = weighted * value if image is None else image + weighted * value
                    light = value * value if light is None else light + value * value
            image_out[p, row, column] = image.reshape(rows, columns)
            light_out[p, row, column] = light.reshape(rows, columns)
        return carry

    lax.fori_loop(0, count * down, body, 0, unroll=2)


def last_body(planes, field, weights, sketches, image_in, light_in, image, light, most):
    odd = lax.rem(lax.axis_index("gx"), 2)
    add_image(odd * (planes - EDGE), EDGE, [(field, weights.at[weights.shape[0] - 1])], sketches,
              (image_in, light_in), image, light)
    breadth, height = light.shape[1:]

    def highest(p):
        return jnp.max(light[p].reshape(breadth // 8, 8, height), axis=0)

    most[...] = lax.fori_loop(1, planes, lambda p, so_far: jnp.maximum(so_far, highest(p)), highest(0))


def divide_body(planes, image, light, most, out, quotient, sems):
    largest = 0.1 * jnp.max(most[...])
    slab = planes // CHUNKS
    copies = []
    for c in range(CHUNKS):
        def body(p, carry):
            quotient[p] = image[p] / (light[p] + largest)
            return carry

        lax.fori_loop(c * slab, (c + 1) * slab, body, 0)
        span = pl.ds(c * slab, slab)
        copies.append(pltpu.make_async_copy(quotient.at[span], out.at[span], sems.at[c]))
        copies[-1].start()
    for copy in copies:
        copy.wait()


def per_device(courant, sketches, probes, source_spot, wavelet, adjoint_before, adjoint_start):
    shots, planes, breadth, height = adjoint_start.shape
    frames, steps = sketches.shape[1], wavelet.shape[1]
    count, areas = lax.axis_size("gx"), lax.axis_size("survey")

    near_pairs = [(i, i ^ 1) for i in range(count)]
    far_pairs = []
    for area in range(areas):
        for i in range(count):
            other = i + 1 if i % 2 else i - 1
            if 0 <= other < count:
                far_pairs.append((area * count + i, area * count + other))
            elif areas % 2 == 0:
                far_pairs.append((area * count + i, (area ^ 1) * count + i))
    plane_bytes = 4 * breadth * height
    whole = held(shots, planes, breadth, height)
    still = held(planes, breadth, height)
    edge = held(EDGE, breadth, height)
    both = held(shots * EDGE, breadth, height)

    def to_far(planes_out):
        return lax.ppermute(planes_out, ("survey", "gx"), far_pairs)

    def to_near(planes_out):
        return lax.ppermute(planes_out, "gx", near_pairs)

    *far, near = call(
        functools.partial(pack_body, shots, planes), (edge,) * shots + (both,), [ANY],
        scratch=[pltpu.SemaphoreType.DMA((2 * shots * EDGE,))], moved=8 * shots * plane_bytes,
    )(in_hbm(adjoint_start))
    far = [to_far(part) for part in far]
    near = to_near(near)
    along_z, along_y, weights, force, edge_force, spot_mask, spot_plane = call(
        functools.partial(tables_body, planes),
        (
            pltpu.VMEM((height, height), BF16), pltpu.VMEM((breadth, 2 * breadth), BF16),
            held(steps, shots, frames, 8, 128), held(steps, shots, 8, 128), held(steps, shots, EDGE, 8, 128),
            held(shots, breadth, height), held(shots, 8, 128),
        ),
        [SMEM] * 3, moved=1 << 20,
    )(source_spot, wavelet, probes)
    images = []
    for instant in range(steps):
        opening, closing = instant == 0, instant == steps - 1
        tables = [along_z, along_y, spot_plane, spot_mask, force, near]
        if opening:
            ahead, near_sent, field, last, courant, sketches = call(
                functools.partial(main_body, shots, planes, 0, False),
                (whole, both, whole, whole, still, pltpu.VMEM(sketches.shape, BF16)), [VMEM] * 6 + [ANY] * 4,
                scratch=[pltpu.SemaphoreType.DMA((3 * CHUNKS + 1,))],
                flops=2 * planes * shots * breadth * height * 512, moved=8 * planes * shots * plane_bytes,
            )(*tables, *(in_hbm(each) for each in (adjoint_start, adjoint_before, courant, sketches)))
        else:
            inputs = [*tables, field, last, courant, weights, sketches, *images]
            ahead, near_sent, *images = call(
                functools.partial(main_body, shots, planes, instant, closing),
                (whole, both, still, still), [VMEM] * len(inputs),
                aliases={len(inputs) - 2: 2, len(inputs) - 1: 3} if images else {},
                flops=2 * planes * shots * breadth * height * 512, moved=8 * planes * shots * plane_bytes,
            )(*inputs)
        if not closing:
            near = to_near(near_sent)
        for shot in range(shots):
            inputs = [along_z, along_y, edge_force, spot_mask, far[shot], field, last, courant, ahead]
            ahead, *sent = call(
                functools.partial(far_body, instant, shot, planes),
                (whole,) if closing else (whole, edge), [VMEM] * len(inputs), aliases={len(inputs) - 1: 0},
                flops=4 * breadth * height * 512, moved=16 * plane_bytes,
            )(*inputs)
            if not closing:
                far[shot] = to_far(sent[0])
        field, last = ahead, field
    image, light, most = call(
        functools.partial(last_body, planes),
        (still, still, held(8, height)), [VMEM] * 5, aliases={3: 0, 4: 1},
        moved=8 * planes * shots * plane_bytes,
    )(field, weights, sketches, *images)
    reach = 1
    while reach < count:
        most = jnp.maximum(most, lax.ppermute(most, "gx", [(i, i ^ reach) for i in range(count)]))
        reach *= 2
    result = call(
        functools.partial(divide_body, planes), pltpu.HBM((planes, breadth, height), F32), [VMEM] * 3,
        scratch=[pltpu.VMEM((planes, breadth, height), F32), pltpu.SemaphoreType.DMA((CHUNKS,))], out_spec=ANY,
        moved=3 * planes * plane_bytes,
    )(image, light, most)
    return result, field


def solution(mesh):
    placed = (
        P("gx", "survey", None),
        P("survey", None, "gx", None, None),
        P("survey", None, None),
        P("survey", None),
        P("survey", None),
        P("survey", "gx", None, None),
        P("survey", "gx", None, None),
    )
    return jax.shard_map(
        per_device,
        mesh=mesh,
        in_specs=placed,
        out_specs=(P("gx", "survey", None), P("survey", "gx", None, None)),
        check_vma=False,
    )
```

```python
import functools

import jax
import jax.numpy as jnp
from jax import lax
from jax.experimental import pallas as pl
from jax.experimental.pallas import tpu as pltpu
from jax.sharding import PartitionSpec as P

F32 = jnp.float32
BF16 = jnp.bfloat16
VMEM = pl.BlockSpec(memory_space=pltpu.VMEM)
SMEM = pl.BlockSpec(memory_space=pltpu.SMEM)
ANY = pl.BlockSpec(memory_space=pl.ANY)
EDGE = 2
CHUNKS = 4


def held(*dims):
    return pltpu.VMEM(dims, F32)


def in_hbm(array):
    return pltpu.with_memory_space_constraint(array, pltpu.HBM)


def call(body, outs, ins, aliases=None, scratch=(), flops=0, moved=0, limit=6 << 20, out_spec=VMEM):
    return pl.pallas_call(
        body,
        out_shape=outs,
        in_specs=ins,
        out_specs=jax.tree.map(lambda _: out_spec, outs),
        scratch_shapes=scratch,
        input_output_aliases=aliases or {},
        compiler_params=pltpu.CompilerParams(vmem_limit_bytes=limit),
        cost_estimate=pl.CostEstimate(flops=flops, bytes_accessed=moved, transcendentals=0),
    )


def orientation(planes, far):
    odd = lax.rem(lax.axis_index("gx"), 2)
    sign = 2 * odd - 1
    base = (1 - odd) * (planes - 1)
    return (base + sign * (planes - 1), -sign) if far else (base, sign)


def pack_body(shots, planes, start, *refs):
    outs, sems = refs[:-1], refs[-1]
    started = []
    for far in (True, False):
        base, sign = orientation(planes, far)
        for s in range(shots):
            for d in range(EDGE):
                target = outs[s].at[d] if far else outs[shots].at[s * EDGE + d]
                copy = pltpu.make_async_copy(start.at[s, base + sign * d], target, sems.at[len(started)])
                copy.start()
                started.append(copy)
    for copy in started:
        copy.wait()


def band(rows, columns, center):
    row = lax.broadcasted_iota(jnp.int32, (rows, columns), 0)
    column = lax.broadcasted_iota(jnp.int32, (rows, columns), 1)
    apart = jnp.abs(row - lax.rem(column, rows))
    return jnp.where(apart == 0, center, jnp.where(apart == 1, 16.0, jnp.where(apart == 2, -1.0, 0.0))).astype(BF16)


def tables_body(planes, spots, wavelet, probes, along_z, along_y, weights, force, edge_force, spot_mask, spot_plane):
    along_z[...] = band(*along_z.shape, -60.0)
    along_y[...] = band(*along_y.shape, -30.0)
    steps, shots, frames = weights.shape[:3]
    base, sign = orientation(planes, False)
    tile = weights.shape[3:]
    for s in range(shots):
        own = (spots[s, 0] - lax.axis_index("gx") * planes - base) * sign
        spot_plane[s] = jnp.full(tile, own, jnp.int32).astype(F32)
        rows = lax.broadcasted_iota(jnp.int32, spot_mask.shape[1:], 0)
        columns = lax.broadcasted_iota(jnp.int32, spot_mask.shape[1:], 1)
        spot_mask[s] = jnp.where((rows == spots[s, 1]) & (columns == spots[s, 2]), 1.0, 0.0)
        for t in range(steps):
            force[t, s] = jnp.full(tile, wavelet[s, t], F32)
            for k in range(EDGE):
                edge_force[t, s, k] = jnp.full(tile, jnp.where(own == planes - 1 - k, wavelet[s, t], 0.0), F32)
            for k in range(frames):
                weights[t, s, k] = jnp.full(tile, probes[s, t, k], F32)


def spread(plane, tile):
    rows, columns = plane.shape
    height, width = tile.shape
    parts = [
        (plane[:, at : at + width].reshape(rows // height, height, width) * tile[None]).reshape(rows, width)
        for at in range(0, columns, width)
    ]
    return jnp.concatenate(parts, axis=1)


def dot(a, b):
    return lax.dot_general(a, b, (((1,), (0,)), ((), ())), preferred_element_type=F32)


def advance(down2, down1, mid, up1, up2, last, scaled, along_z, along_y):
    high = mid.astype(BF16)
    low = (mid - high.astype(F32)).astype(BF16)
    total = dot(high, along_z) + dot(low, along_z) + dot(along_y, jnp.concatenate([high, low], axis=0))
    total = total + (16.0 * (down1 + up1) - (down2 + up2))
    return 2.0 * mid - last + scaled * total


def main_body(shots, planes, instant, closing, *refs):
    refs = list(refs)

    def take(count):
        taken = refs[:count]
        del refs[:count]
        return taken

    opening = instant == 0
    along_z, along_y, spot_plane, spot_mask, force, ghost = take(6)
    if opening:
        sources = take(4)
        ahead, send, field, last, courant, sketches = take(6)
        sems = refs[0]
        slab = planes // CHUNKS
        odd = lax.rem(lax.axis_index("gx"), 2)
        copies = []
        for c in range(CHUNKS):
            first = odd * (c * slab) + (1 - odd) * (planes - slab - c * slab)
            span = pl.ds(first, slab)
            copies.append([
                pltpu.make_async_copy(sources[0].at[:, span], field.at[:, span], sems.at[3 * c]),
                pltpu.make_async_copy(sources[1].at[:, span], last.at[:, span], sems.at[3 * c + 1]),
                pltpu.make_async_copy(sources[2].at[span], courant.at[span], sems.at[3 * c + 2]),
            ])
            for copy in copies[-1]:
                copy.start()
        drawing = pltpu.make_async_copy(sources[3], sketches, sems.at[3 * CHUNKS])
        drawing.start()
    else:
        field, last, courant, weights, sketches = take(5)
        before = take(2) if len(refs) > 4 else None
        ahead, send, image, light = take(4)
    base, sign = orientation(planes, False)

    def at(j):
        return base + sign * j

    def now(s, j):
        return ghost[s * EDGE - 1 - j] if isinstance(j, int) and j < 0 else field[s, at(j)]

    def step(j):
        scaled = courant[at(j)] * (1.0 / 12.0)
        for s in range(shots):
            five = [now(s, j + d) for d in (-2, -1, 0, 1, 2)]
            ahead[s, at(j)] = advance(*five, last[s, at(j)], scaled, along_z[...], along_y[...])

    def body(j, carry):
        step(j)
        return carry

    if opening:
        for c in range(CHUNKS):
            for copy in copies[c]:
                copy.wait()
            if c == 0:
                for j in range(EDGE):
                    step(j)
            low, high = (EDGE, slab - EDGE) if c == 0 else (c * slab - EDGE, (c + 1) * slab - EDGE)
            lax.fori_loop(low, high, body, 0, unroll=2)
    else:
        for j in range(EDGE):
            step(j)
        lax.fori_loop(EDGE, planes - EDGE, body, 0, unroll=2)
    for s in range(shots):
        own = jnp.max(spot_plane[s]).astype(jnp.int32)

        @pl.when((own >= 0) & (own < planes - EDGE))
        def _():
            plane = jnp.clip(at(own), 0, planes - 1)
            ahead[s, plane] = ahead[s, plane] + spread(spot_mask[s], force[instant, s])

    if not closing:
        for s in range(shots):
            for d in range(EDGE):
                send[s * EDGE + d] = ahead[s, at(d)]
    if opening:
        drawing.wait()
    else:
        done = [(field, weights.at[instant - 1])]
        if closing:
            odd = lax.rem(lax.axis_index("gx"), 2)
            ready = done + [(ahead, weights.at[instant])]
            add_image((1 - odd) * EDGE, planes - EDGE, ready, sketches, before, image, light)
            add_image(odd * (planes - EDGE), EDGE, done, sketches, before, image, light)
            send[...] = largest_light((1 - odd) * EDGE, planes - EDGE, light)
        else:
            add_image(0, planes, done, sketches, before, image, light)


def far_body(instant, shot, planes, along_z, along_y, edge_force, spot_mask, ghost, field, last, courant, partial, ahead, *refs):
    base, sign = orientation(planes, True)
    index = lax.axis_index("gx")
    inner = (index > 0) & (index < lax.axis_size("gx") - 1)

    def at(k):
        return base + sign * k

    def now(k):
        return jnp.where(inner, ghost[-1 - k], 0.0) if k < 0 else field[shot, at(k)]

    for k in range(EDGE):
        five = [now(k + d) for d in (-2, -1, 0, 1, 2)]
        value = advance(*five, last[shot, at(k)], courant[at(k)] * (1.0 / 12.0), along_z[...], along_y[...])
        value = value + spread(spot_mask[shot], edge_force[instant, shot, k])
        ahead[shot, at(k)] = value
        if refs:
            refs[0][k] = value


def add_image(low, count, steps, sketches, before, image_out, light_out):
    shots, frames = sketches.shape[:2]
    breadth, height = image_out.shape[1:]
    rows, columns = 16, 128
    down, across = breadth // rows, height // columns

    def tiles(value):
        return value.reshape(rows // 8, 8, columns)

    def body(number, carry):
        p = low + number // down
        row = pl.ds(pl.multiple_of((number % down) * rows, rows), rows)
        for c in range(across):
            column = pl.ds(c * columns, columns)
            image = light = None
            if before is not None:
                image, light = tiles(before[0][p, row, column]), tiles(before[1][p, row, column])
            for s in range(shots):
                drawn = [tiles(sketches[s, k, p, row, column].astype(F32)) for k in range(frames)]
                for field, weights in steps:
                    value = tiles(field[s, p, row, column])
                    weighted = weights[s, 0][None] * drawn[0]
                    for k in range(1, frames):
                        weighted = weighted + weights[s, k][None] * drawn[k]
                    image = weighted * value if image is None else image + weighted * value
                    light = value * value if light is None else light + value * value
            image_out[p, row, column] = image.reshape(rows, columns)
            light_out[p, row, column] = light.reshape(rows, columns)
        return carry

    lax.fori_loop(0, count * down, body, 0, unroll=2)


def largest_light(low, count, light):
    breadth, height = light.shape[1:]

    def highest(p):
        return jnp.max(light[p].reshape(breadth // 8, 8, height), axis=0)

    return lax.fori_loop(1, count, lambda d, most: jnp.maximum(most, highest(low + d)), highest(low))


def last_body(planes, field, weights, sketches, so_far, image_in, light_in, image, light, most):
    odd = lax.rem(lax.axis_index("gx"), 2)
    low = odd * (planes - EDGE)
    add_image(low, EDGE, [(field, weights.at[weights.shape[0] - 1])], sketches, (image_in, light_in), image, light)
    most[...] = jnp.maximum(so_far[...], largest_light(low, EDGE, light))


def divide_body(planes, image, light, most, out, quotient, sems):
    largest = 0.1 * jnp.max(most[...])
    slab = planes // CHUNKS
    copies = []
    for c in range(CHUNKS):
        def body(p, carry):
            quotient[p] = image[p] / (light[p] + largest)
            return carry

        lax.fori_loop(c * slab, (c + 1) * slab, body, 0)
        span = pl.ds(c * slab, slab)
        copies.append(pltpu.make_async_copy(quotient.at[span], out.at[span], sems.at[c]))
        copies[-1].start()
    for copy in copies:
        copy.wait()


def per_device(courant, sketches, probes, source_spot, wavelet, adjoint_before, adjoint_start):
    shots, planes, breadth, height = adjoint_start.shape
    frames, steps = sketches.shape[1], wavelet.shape[1]
    count, areas = lax.axis_size("gx"), lax.axis_size("survey")

    near_pairs = [(i, i ^ 1) for i in range(count)]
    far_pairs = []
    for area in range(areas):
        for i in range(count):
            other = i + 1 if i % 2 else i - 1
            if 0 <= other < count:
                far_pairs.append((area * count + i, area * count + other))
            elif areas % 2 == 0:
                far_pairs.append((area * count + i, (area ^ 1) * count + i))
    plane_bytes = 4 * breadth * height
    whole = held(shots, planes, breadth, height)
    still = held(planes, breadth, height)
    edge = held(EDGE, breadth, height)
    both = held(shots * EDGE, breadth, height)

    def to_far(planes_out):
        return lax.ppermute(planes_out, ("survey", "gx"), far_pairs)

    def to_near(planes_out):
        return lax.ppermute(planes_out, "gx", near_pairs)

    *far, near = call(
        functools.partial(pack_body, shots, planes), (edge,) * shots + (both,), [ANY],
        scratch=[pltpu.SemaphoreType.DMA((2 * shots * EDGE,))], moved=8 * shots * plane_bytes,
    )(in_hbm(adjoint_start))
    far = [to_far(part) for part in far]
    near = to_near(near)
    along_z, along_y, weights, force, edge_force, spot_mask, spot_plane = call(
        functools.partial(tables_body, planes),
        (
            pltpu.VMEM((height, height), BF16), pltpu.VMEM((breadth, 2 * breadth), BF16),
            held(steps, shots, frames, 8, 128), held(steps, shots, 8, 128), held(steps, shots, EDGE, 8, 128),
            held(shots, breadth, height), held(shots, 8, 128),
        ),
        [SMEM] * 3, moved=1 << 20,
    )(source_spot, wavelet, probes)
    images = []
    for instant in range(steps):
        opening, closing = instant == 0, instant == steps - 1
        tables = [along_z, along_y, spot_plane, spot_mask, force, near]
        if opening:
            ahead, near_sent, field, last, courant, sketches = call(
                functools.partial(main_body, shots, planes, 0, False),
                (whole, both, whole, whole, still, pltpu.VMEM(sketches.shape, BF16)), [VMEM] * 6 + [ANY] * 4,
                scratch=[pltpu.SemaphoreType.DMA((3 * CHUNKS + 1,))],
                flops=2 * planes * shots * breadth * height * 512, moved=8 * planes * shots * plane_bytes,
            )(*tables, *(in_hbm(each) for each in (adjoint_start, adjoint_before, courant, sketches)))
        else:
            inputs = [*tables, field, last, courant, weights, sketches, *images]
            ahead, near_sent, *images = call(
                functools.partial(main_body, shots, planes, instant, closing),
                (whole, held(8, height) if closing else both, still, still), [VMEM] * len(inputs),
                aliases={len(inputs) - 2: 2, len(inputs) - 1: 3} if images else {},
                flops=2 * planes * shots * breadth * height * 512, moved=8 * planes * shots * plane_bytes,
            )(*inputs)
        if not closing:
            near = to_near(near_sent)
        for shot in range(shots):
            inputs = [along_z, along_y, edge_force, spot_mask, far[shot], field, last, courant, ahead]
            ahead, *sent = call(
                functools.partial(far_body, instant, shot, planes),
                (whole,) if closing else (whole, edge), [VMEM] * len(inputs), aliases={len(inputs) - 1: 0},
                flops=4 * breadth * height * 512, moved=16 * plane_bytes,
            )(*inputs)
            if not closing:
                far[shot] = to_far(sent[0])
        field, last = ahead, field
    image, light, most = call(
        functools.partial(last_body, planes),
        (still, still, held(8, height)), [VMEM] * 6, aliases={4: 0, 5: 1},
        moved=8 * planes * shots * plane_bytes,
    )(field, weights, sketches, near_sent, *images)
    reach = 1
    while reach < count:
        most = jnp.maximum(most, lax.ppermute(most, "gx", [(i, i ^ reach) for i in range(count)]))
        reach *= 2
    result = call(
        functools.partial(divide_body, planes), pltpu.HBM((planes, breadth, height), F32), [VMEM] * 3,
        scratch=[pltpu.VMEM((planes, breadth, height), F32), pltpu.SemaphoreType.DMA((CHUNKS,))], out_spec=ANY,
        moved=3 * planes * plane_bytes,
    )(image, light, most)
    return result, field


def solution(mesh):
    placed = (
        P("gx", "survey", None),
        P("survey", None, "gx", None, None),
        P("survey", None, None),
        P("survey", None),
        P("survey", None),
        P("survey", "gx", None, None),
        P("survey", "gx", None, None),
    )
    return jax.shard_map(
        per_device,
        mesh=mesh,
        in_specs=placed,
        out_specs=(P("gx", "survey", None), P("survey", "gx", None, None)),
        check_vma=False,
    )
```

```python
import functools

import jax
import jax.numpy as jnp
from jax import lax
from jax.experimental import pallas as pl
from jax.experimental.pallas import tpu as pltpu
from jax.sharding import PartitionSpec as P

F32 = jnp.float32
BF16 = jnp.bfloat16
VMEM = pl.BlockSpec(memory_space=pltpu.VMEM)
SMEM = pl.BlockSpec(memory_space=pltpu.SMEM)
ANY = pl.BlockSpec(memory_space=pl.ANY)
EDGE = 2
WRITES = 8
CHUNKS = 4


def held(*dims):
    return pltpu.VMEM(dims, F32)


def in_hbm(array):
    return pltpu.with_memory_space_constraint(array, pltpu.HBM)


def call(body, outs, ins, aliases=None, scratch=(), flops=0, moved=0, limit=6 << 20, out_spec=VMEM):
    return pl.pallas_call(
        body,
        out_shape=outs,
        in_specs=ins,
        out_specs=jax.tree.map(lambda _: out_spec, outs),
        scratch_shapes=scratch,
        input_output_aliases=aliases or {},
        compiler_params=pltpu.CompilerParams(vmem_limit_bytes=limit),
        cost_estimate=pl.CostEstimate(flops=flops, bytes_accessed=moved, transcendentals=0),
    )


def orientation(planes, far):
    odd = lax.rem(lax.axis_index("gx"), 2)
    sign = 2 * odd - 1
    base = (1 - odd) * (planes - 1)
    return (base + sign * (planes - 1), -sign) if far else (base, sign)


def pack_body(shots, planes, start, *refs):
    outs, sems = refs[:-1], refs[-1]
    started = []
    for far in (True, False):
        base, sign = orientation(planes, far)
        for s in range(shots):
            for d in range(EDGE):
                target = outs[s].at[d] if far else outs[shots].at[s * EDGE + d]
                copy = pltpu.make_async_copy(start.at[s, base + sign * d], target, sems.at[len(started)])
                copy.start()
                started.append(copy)
    for copy in started:
        copy.wait()


def band(rows, columns, center):
    row = lax.broadcasted_iota(jnp.int32, (rows, columns), 0)
    column = lax.broadcasted_iota(jnp.int32, (rows, columns), 1)
    apart = jnp.abs(row - lax.rem(column, rows))
    return jnp.where(apart == 0, center, jnp.where(apart == 1, 16.0, jnp.where(apart == 2, -1.0, 0.0))).astype(BF16)


def tables_body(planes, spots, wavelet, probes, along_z, along_y, weights, force, edge_force, spot_mask, spot_plane):
    along_z[...] = band(*along_z.shape, -60.0)
    along_y[...] = band(*along_y.shape, -30.0)
    steps, shots, frames = weights.shape[:3]
    base, sign = orientation(planes, False)
    tile = weights.shape[3:]
    for s in range(shots):
        own = (spots[s, 0] - lax.axis_index("gx") * planes - base) * sign
        spot_plane[s] = jnp.full(tile, own, jnp.int32).astype(F32)
        rows = lax.broadcasted_iota(jnp.int32, spot_mask.shape[1:], 0)
        columns = lax.broadcasted_iota(jnp.int32, spot_mask.shape[1:], 1)
        spot_mask[s] = jnp.where((rows == spots[s, 1]) & (columns == spots[s, 2]), 1.0, 0.0)
        for t in range(steps):
            force[t, s] = jnp.full(tile, wavelet[s, t], F32)
            for k in range(EDGE):
                edge_force[t, s, k] = jnp.full(tile, jnp.where(own == planes - 1 - k, wavelet[s, t], 0.0), F32)
            for k in range(frames):
                weights[t, s, k] = jnp.full(tile, probes[s, t, k], F32)


def spread(plane, tile):
    rows, columns = plane.shape
    height, width = tile.shape
    parts = [
        (plane[:, at : at + width].reshape(rows // height, height, width) * tile[None]).reshape(rows, width)
        for at in range(0, columns, width)
    ]
    return jnp.concatenate(parts, axis=1)


def dot(a, b):
    return lax.dot_general(a, b, (((1,), (0,)), ((), ())), preferred_element_type=F32)


def advance(down2, down1, mid, up1, up2, last, scaled, along_z, along_y):
    high = mid.astype(BF16)
    low = (mid - high.astype(F32)).astype(BF16)
    total = dot(high, along_z) + dot(low, along_z) + dot(along_y, jnp.concatenate([high, low], axis=0))
    total = total + (16.0 * (down1 + up1) - (down2 + up2))
    return 2.0 * mid - last + scaled * total


def main_body(shots, planes, instant, closing, *refs):
    refs = list(refs)

    def take(count):
        taken = refs[:count]
        del refs[:count]
        return taken

    opening = instant == 0
    along_z, along_y, spot_plane, spot_mask, force, ghost = take(6)
    if opening:
        sources = take(4)
        ahead, send, field, last, courant, sketches = take(6)
        sems = refs[0]
        slab = planes // CHUNKS
        odd = lax.rem(lax.axis_index("gx"), 2)
        copies = []
        for c in range(CHUNKS):
            first = odd * (c * slab) + (1 - odd) * (planes - slab - c * slab)
            span = pl.ds(first, slab)
            copies.append([
                pltpu.make_async_copy(sources[0].at[:, span], field.at[:, span], sems.at[3 * c]),
                pltpu.make_async_copy(sources[1].at[:, span], last.at[:, span], sems.at[3 * c + 1]),
                pltpu.make_async_copy(sources[2].at[span], courant.at[span], sems.at[3 * c + 2]),
            ])
            for copy in copies[-1]:
                copy.start()
        drawing = pltpu.make_async_copy(sources[3], sketches, sems.at[3 * CHUNKS])
        drawing.start()
    else:
        field, last, courant, weights, sketches = take(5)
        before = take(2) if len(refs) > 4 else None
        ahead, send, image, light = take(4)
    base, sign = orientation(planes, False)

    def at(j):
        return base + sign * j

    def now(s, j):
        return ghost[s * EDGE - 1 - j] if isinstance(j, int) and j < 0 else field[s, at(j)]

    def step(j):
        scaled = courant[at(j)] * (1.0 / 12.0)
        for s in range(shots):
            five = [now(s, j + d) for d in (-2, -1, 0, 1, 2)]
            ahead[s, at(j)] = advance(*five, last[s, at(j)], scaled, along_z[...], along_y[...])

    def body(j, carry):
        step(j)
        return carry

    if opening:
        for c in range(CHUNKS):
            for copy in copies[c]:
                copy.wait()
            if c == 0:
                for j in range(EDGE):
                    step(j)
            low, high = (EDGE, slab - EDGE) if c == 0 else (c * slab - EDGE, (c + 1) * slab - EDGE)
            lax.fori_loop(low, high, body, 0, unroll=2)
    else:
        for j in range(EDGE):
            step(j)
        lax.fori_loop(EDGE, planes - EDGE, body, 0, unroll=4)
    for s in range(shots):
        own = jnp.max(spot_plane[s]).astype(jnp.int32)

        @pl.when((own >= 0) & (own < planes - EDGE))
        def _():
            plane = jnp.clip(at(own), 0, planes - 1)
            ahead[s, plane] = ahead[s, plane] + spread(spot_mask[s], force[instant, s])

    if not closing:
        for s in range(shots):
            for d in range(EDGE):
                send[s * EDGE + d] = ahead[s, at(d)]
    if opening:
        drawing.wait()
    else:
        done = [(field, weights.at[instant - 1])]
        if closing:
            odd = lax.rem(lax.axis_index("gx"), 2)
            ready = done + [(ahead, weights.at[instant])]
            add_image((1 - odd) * EDGE, planes - EDGE, ready, sketches, before, image, light)
            add_image(odd * (planes - EDGE), EDGE, done, sketches, before, image, light)
            send[...] = largest_light((1 - odd) * EDGE, planes - EDGE, light)
        else:
            add_image(0, planes, done, sketches, before, image, light)


def far_body(instant, shot, planes, along_z, along_y, edge_force, spot_mask, ghost, field, last, courant, partial, ahead, *refs):
    base, sign = orientation(planes, True)
    index = lax.axis_index("gx")
    inner = (index > 0) & (index < lax.axis_size("gx") - 1)

    def at(k):
        return base + sign * k

    def now(k):
        return jnp.where(inner, ghost[-1 - k], 0.0) if k < 0 else field[shot, at(k)]

    for k in range(EDGE):
        five = [now(k + d) for d in (-2, -1, 0, 1, 2)]
        value = advance(*five, last[shot, at(k)], courant[at(k)] * (1.0 / 12.0), along_z[...], along_y[...])
        value = value + spread(spot_mask[shot], edge_force[instant, shot, k])
        ahead[shot, at(k)] = value
        if refs:
            refs[0][k] = value


def add_image(low, count, steps, sketches, before, image_out, light_out):
    shots, frames = sketches.shape[:2]
    breadth, height = image_out.shape[1:]
    rows, columns = 16, 128
    down, across = breadth // rows, height // columns

    def tiles(value):
        return value.reshape(rows // 8, 8, columns)

    def body(number, carry):
        p = low + number // down
        row = pl.ds(pl.multiple_of((number % down) * rows, rows), rows)
        for c in range(across):
            column = pl.ds(c * columns, columns)
            image = light = None
            if before is not None:
                image, light = tiles(before[0][p, row, column]), tiles(before[1][p, row, column])
            for s in range(shots):
                drawn = [tiles(sketches[s, k, p, row, column].astype(F32)) for k in range(frames)]
                for field, weights in steps:
                    value = tiles(field[s, p, row, column])
                    weighted = weights[s, 0][None] * drawn[0]
                    for k in range(1, frames):
                        weighted = weighted + weights[s, k][None] * drawn[k]
                    image = weighted * value if image is None else image + weighted * value
                    light = value * value if light is None else light + value * value
            image_out[p, row, column] = image.reshape(rows, columns)
            light_out[p, row, column] = light.reshape(rows, columns)
        return carry

    lax.fori_loop(0, count * down, body, 0, unroll=4)


def largest_light(low, count, light):
    breadth, height = light.shape[1:]

    def highest(p):
        return jnp.max(light[p].reshape(breadth // 8, 8, height), axis=0)

    return lax.fori_loop(1, count, lambda d, most: jnp.maximum(most, highest(low + d)), highest(low))


def last_body(planes, field, weights, sketches, so_far, image_in, light_in, image, light, most):
    odd = lax.rem(lax.axis_index("gx"), 2)
    low = odd * (planes - EDGE)
    add_image(low, EDGE, [(field, weights.at[weights.shape[0] - 1])], sketches, (image_in, light_in), image, light)
    most[...] = jnp.maximum(so_far[...], largest_light(low, EDGE, light))


def divide_body(planes, image, light, most, out, quotient, sems):
    largest = 0.1 * jnp.max(most[...])
    slab = planes // WRITES
    copies = []
    for c in range(WRITES):
        def body(p, carry):
            quotient[p] = image[p] / (light[p] + largest)
            return carry

        lax.fori_loop(c * slab, (c + 1) * slab, body, 0)
        span = pl.ds(c * slab, slab)
        copies.append(pltpu.make_async_copy(quotient.at[span], out.at[span], sems.at[c]))
        copies[-1].start()
    for copy in copies:
        copy.wait()


def per_device(courant, sketches, probes, source_spot, wavelet, adjoint_before, adjoint_start):
    shots, planes, breadth, height = adjoint_start.shape
    frames, steps = sketches.shape[1], wavelet.shape[1]
    count, areas = lax.axis_size("gx"), lax.axis_size("survey")

    near_pairs = [(i, i ^ 1) for i in range(count)]
    far_pairs = []
    for area in range(areas):
        for i in range(count):
            other = i + 1 if i % 2 else i - 1
            if 0 <= other < count:
                far_pairs.append((area * count + i, area * count + other))
            elif areas % 2 == 0:
                far_pairs.append((area * count + i, (area ^ 1) * count + i))
    plane_bytes = 4 * breadth * height
    whole = held(shots, planes, breadth, height)
    still = held(planes, breadth, height)
    edge = held(EDGE, breadth, height)
    both = held(shots * EDGE, breadth, height)

    def to_far(planes_out):
        return lax.ppermute(planes_out, ("survey", "gx"), far_pairs)

    def to_near(planes_out):
        return lax.ppermute(planes_out, "gx", near_pairs)

    *far, near = call(
        functools.partial(pack_body, shots, planes), (edge,) * shots + (both,), [ANY],
        scratch=[pltpu.SemaphoreType.DMA((2 * shots * EDGE,))], moved=8 * shots * plane_bytes,
    )(in_hbm(adjoint_start))
    far = [to_far(part) for part in far]
    near = to_near(near)
    along_z, along_y, weights, force, edge_force, spot_mask, spot_plane = call(
        functools.partial(tables_body, planes),
        (
            pltpu.VMEM((height, height), BF16), pltpu.VMEM((breadth, 2 * breadth), BF16),
            held(steps, shots, frames, 8, 128), held(steps, shots, 8, 128), held(steps, shots, EDGE, 8, 128),
            held(shots, breadth, height), held(shots, 8, 128),
        ),
        [SMEM] * 3, moved=1 << 20,
    )(source_spot, wavelet, probes)
    images = []
    for instant in range(steps):
        opening, closing = instant == 0, instant == steps - 1
        tables = [along_z, along_y, spot_plane, spot_mask, force, near]
        if opening:
            ahead, near_sent, field, last, courant, sketches = call(
                functools.partial(main_body, shots, planes, 0, False),
                (whole, both, whole, whole, still, pltpu.VMEM(sketches.shape, BF16)), [VMEM] * 6 + [ANY] * 4,
                scratch=[pltpu.SemaphoreType.DMA((3 * CHUNKS + 1,))],
                flops=2 * planes * shots * breadth * height * 512, moved=8 * planes * shots * plane_bytes,
            )(*tables, *(in_hbm(each) for each in (adjoint_start, adjoint_before, courant, sketches)))
        else:
            inputs = [*tables, field, last, courant, weights, sketches, *images]
            ahead, near_sent, *images = call(
                functools.partial(main_body, shots, planes, instant, closing),
                (whole, held(8, height) if closing else both, still, still), [VMEM] * len(inputs),
                aliases={len(inputs) - 2: 2, len(inputs) - 1: 3} if images else {},
                flops=2 * planes * shots * breadth * height * 512, moved=8 * planes * shots * plane_bytes,
            )(*inputs)
        if not closing:
            near = to_near(near_sent)
        for shot in range(shots):
            inputs = [along_z, along_y, edge_force, spot_mask, far[shot], field, last, courant, ahead]
            ahead, *sent = call(
                functools.partial(far_body, instant, shot, planes),
                (whole,) if closing else (whole, edge), [VMEM] * len(inputs), aliases={len(inputs) - 1: 0},
                flops=4 * breadth * height * 512, moved=16 * plane_bytes,
            )(*inputs)
            if not closing:
                far[shot] = to_far(sent[0])
        field, last = ahead, field
    image, light, most = call(
        functools.partial(last_body, planes),
        (still, still, held(8, height)), [VMEM] * 6, aliases={4: 0, 5: 1},
        moved=8 * planes * shots * plane_bytes,
    )(field, weights, sketches, near_sent, *images)
    reach = 1
    while reach < count:
        most = jnp.maximum(most, lax.ppermute(most, "gx", [(i, i ^ reach) for i in range(count)]))
        reach *= 2
    result = call(
        functools.partial(divide_body, planes), pltpu.HBM((planes, breadth, height), F32), [VMEM] * 3,
        scratch=[pltpu.VMEM((planes, breadth, height), F32), pltpu.SemaphoreType.DMA((WRITES,))], out_spec=ANY,
        moved=3 * planes * plane_bytes,
    )(image, light, most)
    return result, field


def solution(mesh):
    placed = (
        P("gx", "survey", None),
        P("survey", None, "gx", None, None),
        P("survey", None, None),
        P("survey", None),
        P("survey", None),
        P("survey", "gx", None, None),
        P("survey", "gx", None, None),
    )
    return jax.shard_map(
        per_device,
        mesh=mesh,
        in_specs=placed,
        out_specs=(P("gx", "survey", None), P("survey", "gx", None, None)),
        check_vma=False,
    )
```
